32 devices in a mesh: dp: 8 (over y, x, core), seq: 4 (over z).
Axes of the slice: x: 2, y: 2, z: 4, core: 2. Of those that a mesh axis runs over, the one named last changes fastest.
Arguments:
- hidden_in: bfloat16 [24, 2048, 1024], P('dp', 'seq'), may hold values from -6 to 6
- cotangent: bfloat16 [24, 2048, 1024], P('dp', 'seq'), may hold values from -6 to 6
- first_gain: bfloat16 [1024], P(('dp', 'seq')), may hold values from 0.099609375 to 1.8984375
- first_shift: bfloat16 [1024], P(('dp', 'seq')), may hold values from -3 to 3
- triple_weight: bfloat16 [1024, 3072], P(('dp', 'seq')), may hold values from -0.1875 to 0.1875
- triple_bias: bfloat16 [3072], P(('dp', 'seq')), may hold values from -3 to 3
- dense_weight: bfloat16 [1024, 1024], P(('dp', 'seq')), may hold values from -0.75 to 0.75
- dense_bias: bfloat16 [1024], P(('dp', 'seq')), may hold values from -3 to 3
- second_gain: bfloat16 [1024], P(('dp', 'seq')), may hold values from 0.099609375 to 1.8984375
- second_shift: bfloat16 [1024], P(('dp', 'seq')), may hold values from -3 to 3
- expand_weight: bfloat16 [1024, 4096], P(('dp', 'seq')), may hold values from -0.1875 to 0.1875
- expand_bias: bfloat16 [4096], P(('dp', 'seq')), may hold values from -3 to 3
- contract_weight: bfloat16 [4096, 1024], P(('dp', 'seq')), may hold values from -0.09375 to 0.09375
- contract_bias: bfloat16 [1024], P(('dp', 'seq')), may hold values from -3 to 3
Outputs:
- block_out: bfloat16 [24, 2048, 1024], P('dp', 'seq')
- grad_input: float32 [24, 2048, 1024], P('dp', 'seq')
- grad_first_gain: float32 [1024], P(('dp', 'seq'))
- grad_first_shift: float32 [1024], P(('dp', 'seq'))
- grad_triple_weight: float32 [1024, 3072], P(('dp', 'seq'))
- grad_triple_bias: float32 [3072], P(('dp', 'seq'))
- grad_dense_weight: float32 [1024, 1024], P(('dp', 'seq'))
- grad_dense_bias: float32 [1024], P(('dp', 'seq'))
- grad_second_gain: float32 [1024], P(('dp', 'seq'))
- grad_second_shift: float32 [1024], P(('dp', 'seq'))
- grad_expand_weight: float32 [1024, 4096], P(('dp', 'seq'))
- grad_expand_bias: float32 [4096], P(('dp', 'seq'))
- grad_contract_weight: float32 [4096, 1024], P(('dp', 'seq'))
- grad_contract_bias: float32 [1024], P(('dp', 'seq'))
The draws below stay inside these ranges and needn't reach their ends.
All inputs are finite; a program needn't handle non-finite values.
Results may differ from the reference program's by a relative error of at most 0.0098.
Values may be sent and summed in bfloat16 or wider, within the bound.
A program may use at most 448 MiB of HBM per device.

```python
import math
import jax
import jax.numpy as jnp
from jax import lax

D = 1024
H = 16
HD = 64
FF = 4096
ROT = 16
LEN = 2048
SEQS = 24


def steps_of(own_key, shape, split, smallest, top_value):
    def one(axis_at, blocks):
        heights = jax.random.uniform(jax.random.fold_in(jax.random.fold_in(own_key, 6), axis_at), (blocks,), jnp.float32, smallest / len(split), top_value / len(split))
        return jnp.repeat(jnp.exp(heights), shape[axis_at] // blocks).reshape((-1,) + (1,) * (len(shape) - axis_at - 1))

    loudness = one(*split[0])
    for cut in split[1:]:
        loudness = loudness * one(*cut)
    return loudness


def bell_draw(key, extent, spread, most, cuts=(), held_as=jnp.bfloat16):
    values = spread * jax.random.normal(key, extent, jnp.float32)
    if cuts:
        values = values * steps_of(key, extent, cuts, -0.22, 0.18)
    return jnp.clip(values, -most, most).astype(held_as)


def setup_inputs(seed: int = 0) -> dict:
    streams_of = jax.random.split(jax.random.key(seed), 15)
    hidden_in = bell_draw(streams_of[0], (SEQS, LEN, D), 1.0, 6.0, ((0, 8), (1, 4)))
    cotangent = bell_draw(streams_of[1], (SEQS, LEN, D), 1.0, 6.0, ((0, 8), (1, 4)))
    first_gain = jnp.clip(1.0 + 0.18 * jax.random.normal(streams_of[2], (D,), jnp.float32), 0.099609375, 1.8984375).astype(jnp.bfloat16)
    first_shift = bell_draw(streams_of[3], (D,), 0.5, 3.0, ((0, 32),))
    triple_weight = bell_draw(streams_of[4], (D, 3 * D), D ** -0.5, 0.1875, ((0, 32),))
    triple_bias = bell_draw(streams_of[5], (3 * D,), 0.5, 3.0, ((0, 32),))
    dense_weight = bell_draw(streams_of[6], (D, D), (D // 16) ** -0.5, 0.75, ((0, 32),))
    dense_bias = bell_draw(streams_of[7], (D,), 0.5, 3.0, ((0, 32),))
    second_gain = jnp.clip(1.0 + 0.18 * jax.random.normal(streams_of[8], (D,), jnp.float32), 0.099609375, 1.8984375).astype(jnp.bfloat16)
    second_shift = bell_draw(streams_of[9], (D,), 0.5, 3.0, ((0, 32),))
    expand_weight = bell_draw(streams_of[10], (D, FF), D ** -0.5, 0.1875, ((0, 32),))
    expand_bias = bell_draw(streams_of[11], (FF,), 0.5, 3.0, ((0, 32),))
    contract_weight = bell_draw(streams_of[12], (FF, D), FF ** -0.5, 0.09375, ((0, 32),))
    contract_bias = bell_draw(streams_of[13], (D,), 0.5, 3.0, ((0, 32),))
    return dict(hidden_in=hidden_in, cotangent=cotangent, first_gain=first_gain, first_shift=first_shift, triple_weight=triple_weight, triple_bias=triple_bias, dense_weight=dense_weight, dense_bias=dense_bias, second_gain=second_gain, second_shift=second_shift, expand_weight=expand_weight, expand_bias=expand_bias, contract_weight=contract_weight, contract_bias=contract_bias)


top_precision = lax.Precision.HIGHEST
big_negative = -1e+30
epsilon = 1e-05

@jax.custom_vjp
def low(v):
    return lax.optimization_barrier(v.astype(jnp.bfloat16)).astype(jnp.float32)

@jax.custom_vjp
def low_back(v):
    return v

def low_keep(v):
    return (low(v), None)

def low_pass(kept, grad):
    return (grad,)

def back_keep(v):
    return (v, None)

def back_low(kept, grad):
    return (low(grad),)
low.defvjp(low_keep, low_pass)
low_back.defvjp(back_keep, back_low)

def layer_norm(values, gain, shift):
    average = lax.optimization_barrier(jnp.mean(values, axis=-1, keepdims=True))
    centered = values - average
    variance = lax.optimization_barrier(jnp.mean(centered * centered, axis=-1, keepdims=True))
    return centered * lax.rsqrt(variance + epsilon) * gain + shift

def rotary_tables(positions, rotary):
    half = rotary // 2
    frequency = 10000.0 ** (-(jnp.arange(half, dtype=jnp.float32) * 2.0 / rotary))
    angles = positions.astype(jnp.float32)[:, None] * frequency[None, :]
    angles = jnp.concatenate([angles, angles], axis=-1)
    return (jnp.cos(angles), jnp.sin(angles))

def rotate(values, cosine, sine):
    rotary = cosine.shape[-1]
    half = rotary // 2
    leading = values[..., :rotary]
    turned = jnp.concatenate([-leading[..., half:], leading[..., :half]], axis=-1)
    return jnp.concatenate([leading * cosine + turned * sine, values[..., rotary:]], axis=-1)

def attend(query, keys, values, block, scale):
    group, length, heads, depth = query.shape
    count = length // block

    def one_block(pieces):
        query_block, start = pieces
        scores = jnp.einsum('gbhe,glhe->ghbl', query_block, keys, precision=top_precision) * scale
        scores = low_back(scores)
        rows = start + lax.broadcasted_iota(jnp.int32, (block, length), 0)
        columns = lax.broadcasted_iota(jnp.int32, (block, length), 1)
        masked = jnp.where(columns <= rows, scores, big_negative)
        highest = lax.optimization_barrier(jnp.max(masked, axis=-1, keepdims=True))
        weights = jnp.exp(masked - highest)
        total = lax.optimization_barrier(jnp.sum(weights, axis=-1, keepdims=True))
        probability = low(weights / total)
        return jnp.einsum('ghbl,glhe->gbhe', probability, values, precision=top_precision)
    blocks = query.reshape(group, count, block, heads, depth).transpose(1, 0, 2, 3, 4)
    starts = jnp.arange(count, dtype=jnp.int32) * block
    outputs = lax.map(jax.checkpoint(one_block), (blocks, starts))
    return outputs.transpose(1, 0, 2, 3, 4).reshape(group, length, heads, depth)

def forward(params, source):
    first_gain, first_shift, triple_weight, triple_bias, dense_weight, dense_bias, second_gain, second_shift, expand_weight, expand_bias, contract_weight, contract_bias = params
    group, length, width = source.shape
    normed_one = low(layer_norm(source, first_gain, first_shift))
    normed_two = low(layer_norm(source, second_gain, second_shift))
    triple = jnp.einsum('gld,de->gle', normed_one, triple_weight, precision=top_precision) + triple_bias
    triple = low_back(triple).reshape(group, length, 3, H, HD)
    cosine, sine = rotary_tables(jnp.arange(length, dtype=jnp.int32), ROT)
    cosine = cosine[:, None, :]
    sine = sine[:, None, :]
    query = low_back(low(rotate(triple[:, :, 0], cosine, sine)))
    keys = low_back(low(rotate(triple[:, :, 1], cosine, sine)))
    values = low_back(low(triple[:, :, 2]))
    block = 512 if length % 512 == 0 else length
    context = attend(query, keys, values, block, 1.0 / math.sqrt(HD))
    context = low_back(low(context)).reshape(group, length, width)
    attended = jnp.einsum('gld,de->gle', context, dense_weight, precision=top_precision) + dense_bias
    expanded = low_back(jnp.einsum('gld,df->glf', normed_two, expand_weight, precision=top_precision) + expand_bias)
    activated = low(jax.nn.gelu(expanded, approximate=False))
    contracted = jnp.einsum('glf,fd->gld', activated, contract_weight, precision=top_precision) + contract_bias
    return source + attended + contracted

def reference(hidden_in, cotangent, first_gain, first_shift, triple_weight, triple_bias, dense_weight, dense_bias, second_gain, second_shift, expand_weight, expand_bias, contract_weight, contract_bias):
    params = tuple((item.astype(jnp.float32) for item in (first_gain, first_shift, triple_weight, triple_bias, dense_weight, dense_bias, second_gain, second_shift, expand_weight, expand_bias, contract_weight, contract_bias)))
    total_seqs, length, width = hidden_in.shape
    group = 2 if total_seqs % 2 == 0 else 1
    count = total_seqs // group
    sources = hidden_in.astype(jnp.float32).reshape(count, group, length, width)
    upstreams = cotangent.astype(jnp.float32).reshape(count, group, length, width)

    def one_group(carry, pieces):
        source, upstream = pieces
        output, pullback = jax.vjp(forward, params, source)
        grad_params, grad_source = pullback(upstream)
        carry = jax.tree.map(lambda left, right: left + right, carry, grad_params)
        return (carry, (output.astype(jnp.bfloat16), grad_source))
    zeros = jax.tree.map(jnp.zeros_like, params)
    totals, (outputs, grad_sources) = lax.scan(one_group, zeros, (sources, upstreams))
    return (outputs.reshape(total_seqs, length, width), grad_sources.reshape(total_seqs, length, width), totals[0], totals[1], totals[2], totals[3], totals[4], totals[5], totals[6], totals[7], totals[8], totals[9], totals[10], totals[11])
```

```python
import math

import jax
import jax.numpy as jnp
from jax import lax
from jax.experimental import pallas as pl
from jax.experimental.pallas import tpu as pltpu
from jax.sharding import PartitionSpec as P

H = 16
HD = 64
ROT = 16


big_negative = -1e30
epsilon = 1e-05


def layer_norm(values, gain, shift):
    average = jnp.mean(values, axis=-1, keepdims=True)
    centered = values - average
    variance = jnp.mean(centered * centered, axis=-1, keepdims=True)
    return centered * lax.rsqrt(variance + epsilon) * gain + shift


def rotary_tables(positions, width):
    half = ROT // 2
    entry = jnp.arange(HD, dtype=jnp.int32)
    index = (entry % half).astype(jnp.float32)
    frequency = 10000.0 ** (-(index * 2.0 / ROT))
    angles = positions.astype(jnp.float32)[:, None] * frequency[None, :]
    cosine, sine = jnp.cos(angles), jnp.sin(angles)
    keep = jnp.where(entry < ROT, cosine, 1.0)
    ahead = jnp.where(entry < half, -sine, 0.0)
    behind = jnp.where((entry >= half) & (entry < ROT), sine, 0.0)
    return tuple(jnp.tile(table, (1, width // HD)) for table in (keep, ahead, behind))


def turn(values, keep, ahead, behind, sign):
    half = ROT // 2
    width = values.shape[-1]
    return values * keep + sign * (
        pltpu.roll(values, width - half, 1) * ahead + pltpu.roll(values, half, 1) * behind
    )


NT = (((1,), (1,)), ((), ()))


def project_body(
    h_ref, y_ref, wq_ref, wk_ref, wv_ref, wd_ref, bq_ref, bk_ref, bv_ref, keep, ahead, behind, out_ref
):
    h = h_ref[...]
    for slot, w_ref, b_ref in ((0, wq_ref, bq_ref), (1, wk_ref, bk_ref)):
        t = jnp.dot(h, w_ref[...], preferred_element_type=jnp.float32) + b_ref[...]
        out_ref[slot] = turn(t, keep[...], ahead[...], behind[...], 1.0).astype(jnp.bfloat16)
    t = jnp.dot(h, wv_ref[...], preferred_element_type=jnp.float32) + bv_ref[...]
    out_ref[2] = t.astype(jnp.bfloat16)
    dc = lax.dot_general(y_ref[...], wd_ref[...], NT, preferred_element_type=jnp.float32)
    out_ref[3] = dc.astype(jnp.bfloat16)


def project(which, low_one, upstream, weights, bias, tables, part_len, groups):
    width = low_one.shape[1]
    mine = width // groups

    def columns(block):
        return pl.BlockSpec((width, mine), lambda g, b=block: (0, b * groups + g))

    def biases(block):
        return pl.BlockSpec((1, mine), lambda g, b=block: (0, b * groups + g))

    rows = pl.BlockSpec((part_len, width), lambda g: (which, 0))
    table = pl.BlockSpec((part_len, mine), lambda g: (0, 0))
    return pl.pallas_call(
        project_body,
        grid=(groups,),
        in_specs=[
            rows,
            rows,
            columns(0),
            columns(1),
            columns(2),
            pl.BlockSpec((mine, width), lambda g: (g, 3)),
            biases(0),
            biases(1),
            biases(2),
            table,
            table,
            table,
        ],
        out_specs=pl.BlockSpec((None, 4, part_len, mine), lambda g: (g, 0, 0, 0)),
        out_shape=jax.ShapeDtypeStruct((groups, 4, part_len, mine), jnp.bfloat16),
        compiler_params=pltpu.CompilerParams(
            dimension_semantics=("arbitrary",), vmem_limit_bytes=40 * 1024 * 1024
        ),
        cost_estimate=pl.CostEstimate(
            flops=8 * part_len * width * width,
            bytes_accessed=2 * (4 * width * width + 6 * part_len * width),
            transcendentals=0,
        ),
        name="project",
    )(
        low_one,
        upstream,
        weights,
        weights,
        weights,
        weights,
        bias,
        bias,
        bias,
        *tables,
    )


def attention_body(
    heads, block, q_ref, k_ref, v_ref, dc_ref, out_ref, s_ref, dk_acc, dv_acc, kt_ref, vt_ref
):
    qi = pl.program_id(0)
    steps = pl.num_programs(0)
    scale = 1.0 / math.sqrt(HD)
    width = heads * HD

    @pl.when(qi == 0)
    def _():
        dk_acc[...] = jnp.zeros_like(dk_acc)
        dv_acc[...] = jnp.zeros_like(dv_acc)

        @pl.loop(0, steps)
        def _(ki):
            kt_ref[ki] = k_ref[ki].T
            vt_ref[ki] = v_ref[ki].T

    lane = lax.broadcasted_iota(jnp.int32, (block, width), 1) // HD
    causal = lax.broadcasted_iota(jnp.int32, (block, block), 0) <= lax.broadcasted_iota(
        jnp.int32, (block, block), 1
    )
    q_all = q_ref[...] * jnp.bfloat16(scale)
    dc_all = dc_ref[...]
    contexts = []
    grads = []
    for h in range(heads):
        zero = jnp.zeros_like(q_all)
        q = jnp.where(lane == h, q_all, zero)
        dc = jnp.where(lane == h, dc_all, zero)
        rows = pl.ds(h * HD, HD)

        def scores(ki, q=q):
            return lax.dot_general(k_ref[ki], q, NT, preferred_element_type=jnp.float32)

        def first(ki, highest, scores=scores):
            s = scores(ki)
            s_ref[ki] = s
            return jnp.maximum(highest, jnp.max(s, axis=0, keepdims=True))

        diagonal = jnp.where(causal, scores(qi), big_negative)
        s_ref[qi] = diagonal
        highest = lax.fori_loop(0, qi, first, jnp.max(diagonal, axis=0, keepdims=True))

        def second(ki, carry, highest=highest, rows=rows):
            total, context = carry
            e = jnp.exp(s_ref[ki] - highest)
            total = total + jnp.sum(e, axis=0, keepdims=True)
            context = context + jnp.dot(
                vt_ref[ki, rows, :], e.astype(jnp.bfloat16), preferred_element_type=jnp.float32
            )
            return (total, context)

        total, context = lax.fori_loop(
            0,
            qi + 1,
            second,
            (jnp.zeros((1, block), jnp.float32), jnp.zeros((HD, block), jnp.float32)),
        )
        context = context / total
        log_total = highest + jnp.log(total)
        contexts.append(context)
        dct = dc_all[:, h * HD : (h + 1) * HD].astype(jnp.float32).T
        inner = jnp.sum(context * dct, axis=0, keepdims=True)

        def third(ki, grad, q=q, dc=dc, inner=inner, log_total=log_total, rows=rows):
            p = jnp.exp(s_ref[ki] - log_total)
            dp = lax.dot_general(v_ref[ki], dc, NT, preferred_element_type=jnp.float32)
            ds = (p * (dp - inner)).astype(jnp.bfloat16)
            dv_acc[ki] += jnp.dot(p.astype(jnp.bfloat16), dc, preferred_element_type=jnp.float32)
            dk_acc[ki] += jnp.dot(ds, q, preferred_element_type=jnp.float32)
            return grad + jnp.dot(kt_ref[ki, rows, :], ds, preferred_element_type=jnp.float32)

        grad = lax.fori_loop(0, qi + 1, third, jnp.zeros((HD, block), jnp.float32))
        grads.append(grad * scale)
    out_ref[qi, 0] = jnp.concatenate(contexts, axis=0).T.astype(jnp.bfloat16)
    out_ref[qi, 1] = jnp.concatenate(grads, axis=0).T.astype(jnp.bfloat16)

    @pl.when(qi == steps - 1)
    def _():
        @pl.loop(0, steps)
        def _(ki):
            out_ref[ki, 2] = dk_acc[ki].astype(jnp.bfloat16)
            out_ref[ki, 3] = dv_acc[ki].astype(jnp.bfloat16)


def attention(parts):
    groups, _, block, width = parts.shape
    heads = width // HD
    length = groups * block

    def rows_of(which):
        return pl.BlockSpec((None, None, block, width), lambda i, w=which: (i, w, 0, 0))

    def whole_of(which):
        return pl.BlockSpec((groups, None, block, width), lambda i, w=which: (0, w, 0, 0))

    def body(*refs):
        attention_body(heads, block, *refs)

    return pl.pallas_call(
        body,
        grid=(groups,),
        in_specs=[rows_of(0), whole_of(1), whole_of(2), rows_of(3)],
        out_specs=pl.BlockSpec(parts.shape, lambda i: (0, 0, 0, 0)),
        out_shape=jax.ShapeDtypeStruct(parts.shape, jnp.bfloat16),
        scratch_shapes=[
            pltpu.VMEM((groups, block, block), jnp.float32),
            pltpu.VMEM((groups, block, width), jnp.float32),
            pltpu.VMEM((groups, block, width), jnp.float32),
            pltpu.VMEM((groups, width, block), jnp.bfloat16),
            pltpu.VMEM((groups, width, block), jnp.bfloat16),
        ],
        compiler_params=pltpu.CompilerParams(
            dimension_semantics=("arbitrary",), vmem_limit_bytes=50 * 1024 * 1024
        ),
        cost_estimate=pl.CostEstimate(
            flops=32 * heads * length * length * HD,
            bytes_accessed=16 * length * width,
            transcendentals=heads * length * length,
        ),
        name="attention",
    )(parts, parts, parts, parts)


def finish_body(
    groups,
    mine,
    chained,
    r_ref,
    w_ref,
    x_ref,
    f_ref,
    g_ref,
    gain_ref,
    bias_ref,
    keep,
    ahead,
    behind,
    *refs,
):
    out_ref, grad_ref, dt_ref, c_ref, gain_sum, shift_sum, bias_sum = refs[chained:]
    width = groups * mine

    @pl.when(pl.program_id(0) == 0)
    def _():
        gain_sum[...] = jnp.zeros_like(gain_sum)
        shift_sum[...] = jnp.zeros_like(shift_sum)
        bias_sum[...] = jnp.zeros_like(bias_sum)

    x = x_ref[...].astype(jnp.float32)
    for g in range(groups):
        at = g * mine
        c_ref[:, at : at + mine] = r_ref[g, 0]
        for slot in (1, 2):
            turned = turn(
                r_ref[g, slot].astype(jnp.float32), keep[...], ahead[...], behind[...], -1.0
            ).astype(jnp.bfloat16)
            here = (slot - 1) * width + at
            dt_ref[:, here : here + mine] = turned
        dt_ref[:, 2 * width + at : 2 * width + at + mine] = r_ref[g, 3]
    attended = jnp.dot(
        c_ref[...], w_ref[:, 3 * width : 4 * width], preferred_element_type=jnp.float32
    )
    out_ref[...] = (x + (attended + bias_ref[...]) + f_ref[...]).astype(jnp.bfloat16)
    dt = dt_ref[...]
    bias_sum[...] += jnp.sum(dt.astype(jnp.float32), axis=0, keepdims=True)
    dh = lax.dot_general(dt, w_ref[:, : 3 * width], NT, preferred_element_type=jnp.float32)
    average = jnp.mean(x, axis=-1, keepdims=True)
    centered = x - average
    inverse = lax.rsqrt(jnp.mean(centered * centered, axis=-1, keepdims=True) + epsilon)
    xh = centered * inverse
    gain_sum[...] += jnp.sum(dh * xh, axis=0, keepdims=True)
    shift_sum[...] += jnp.sum(dh, axis=0, keepdims=True)
    dg = dh * gain_ref[...]
    first = jnp.mean(dg, axis=-1, keepdims=True)
    second = jnp.mean(dg * xh, axis=-1, keepdims=True)
    grad_ref[...] = g_ref[...] + (dg - first - xh * second) * inverse


def finish(which, returned, weights, hidden, contracted, partial, gain, bias, tables, chain):
    groups, _, part_len, mine = returned.shape
    seqs, _, width = hidden.shape
    block = min(256, part_len)
    chain = tuple(chain)

    def row(size):
        return pl.BlockSpec((1, size), lambda j: (0, 0))

    tokens = pl.BlockSpec((None, block, width), lambda j: (which, j, 0))
    triple = pl.BlockSpec((None, block, 3 * width), lambda j: (which, j, 0))
    table = pl.BlockSpec((block, mine), lambda j: (j, 0))
    ordinary = 10

    def body(*refs):
        finish_body(groups, mine, len(chain), *refs)

    return pl.pallas_call(
        body,
        grid=(part_len // block,),
        in_specs=[
            pl.BlockSpec((groups, 4, block, mine), lambda j: (0, 0, j, 0)),
            pl.BlockSpec(weights.shape, lambda j: (0, 0)),
            tokens,
            tokens,
            tokens,
            row(width),
            row(width),
            table,
            table,
            table,
        ]
        + [pl.BlockSpec(memory_space=pl.ANY)] * len(chain),
        out_specs=[tokens, tokens, triple, tokens, row(width), row(width), row(3 * width)],
        out_shape=[
            jax.ShapeDtypeStruct((seqs, part_len, width), jnp.bfloat16),
            jax.ShapeDtypeStruct((seqs, part_len, width), jnp.float32),
            jax.ShapeDtypeStruct((seqs, part_len, 3 * width), jnp.bfloat16),
            jax.ShapeDtypeStruct((seqs, part_len, width), jnp.bfloat16),
            jax.ShapeDtypeStruct((1, width), jnp.float32),
            jax.ShapeDtypeStruct((1, width), jnp.float32),
            jax.ShapeDtypeStruct((1, 3 * width), jnp.float32),
        ],
        input_output_aliases={ordinary + i: i for i in range(len(chain))},
        compiler_params=pltpu.CompilerParams(
            dimension_semantics=("arbitrary",), vmem_limit_bytes=56 * 1024 * 1024
        ),
        cost_estimate=pl.CostEstimate(
            flops=8 * part_len * width * width,
            bytes_accessed=2 * (4 * width * width + 14 * part_len * width),
            transcendentals=0,
        ),
        name="finish",
    )(returned, weights, hidden, contracted, partial, gain, bias, *tables, *chain)


def scatter_sum(values):
    values = lax.psum_scatter(values, "dp", scatter_dimension=0, tiled=True)
    return lax.psum_scatter(values, "seq", scatter_dimension=0, tiled=True)


def local(
    hidden_in,
    cotangent,
    first_gain,
    first_shift,
    triple_weight,
    triple_bias,
    dense_weight,
    dense_bias,
    second_gain,
    second_shift,
    expand_weight,
    expand_bias,
    contract_weight,
    contract_bias,
):
    axes = ("dp", "seq")
    devices = lax.axis_size("dp") * lax.axis_size("seq")
    groups = lax.axis_size("seq")
    seqs, part_len, width = hidden_in.shape
    tokens_here = seqs * part_len
    shard = triple_weight.shape[0]
    vectors = (
        first_gain,
        first_shift,
        triple_bias,
        dense_bias,
        second_gain,
        second_shift,
        expand_bias,
        contract_bias,
    )
    columns = [vector.reshape(shard, -1) for vector in vectors]
    used = sum(column.shape[1] for column in columns)
    padding = jnp.zeros((shard, 128 - used), jnp.bfloat16)
    w_near = lax.all_gather(
        jnp.concatenate([triple_weight, dense_weight, *columns, padding], axis=1),
        axes,
        axis=0,
        tiled=True,
    )
    stacked = w_near[:, 4 * width : 4 * width + used].astype(jnp.float32)
    whole = []
    offset = 0
    for column in columns:
        size = column.shape[1]
        whole.append(stacked[:, offset : offset + size].reshape(-1))
        offset += size
    gain_one, shift_one, b_triple, b_dense, gain_two, shift_two, b_expand, b_contract = whole
    w_expand = lax.all_gather(expand_weight, axes, axis=0, tiled=True)
    w_contract = lax.all_gather(contract_weight, axes, axis=0, tiled=True)
    source = hidden_in.astype(jnp.float32).reshape(tokens_here, width)
    upstream = cotangent.reshape(tokens_here, width)
    low_one = layer_norm(source, gain_one, shift_one).astype(jnp.bfloat16)
    normed_two, pull_two = jax.vjp(layer_norm, source, gain_two, shift_two)
    low_two = normed_two.astype(jnp.bfloat16)
    positions = lax.axis_index("seq") * part_len + jnp.arange(part_len, dtype=jnp.int32)
    tables = rotary_tables(positions, width // groups)
    received = []
    for which in range(seqs):
        sending = project(
            which, low_one, upstream, w_near, b_triple[None], tables, part_len, groups
        )
        received.append(
            lax.all_to_all(sending, "seq", split_axis=0, concat_axis=0, tiled=True)
        )
    returned = []
    for which in range(seqs):
        outcome = attention(received[which])
        returned.append(
            lax.all_to_all(outcome, "seq", split_axis=0, concat_axis=0, tiled=True)
        )
    expanded = jnp.dot(low_two, w_expand, preferred_element_type=jnp.float32) + b_expand
    activated, pull_gelu = jax.vjp(lambda inner: jax.nn.gelu(inner, approximate=False), expanded)
    low_act = activated.astype(jnp.bfloat16)
    contracted = (
        jnp.dot(low_act, w_contract, preferred_element_type=jnp.float32) + b_contract
    )
    upstream_total = jnp.sum(upstream.astype(jnp.float32), axis=0)
    grad_act = jnp.einsum("td,fd->tf", upstream, w_contract, preferred_element_type=jnp.float32)
    grad_expanded = pull_gelu(grad_act)[0].astype(jnp.bfloat16)
    grad_w_contract = jnp.einsum("tf,td->fd", low_act, upstream, preferred_element_type=jnp.float32)
    grad_w_expand = jnp.einsum(
        "td,tf->df", low_two, grad_expanded, preferred_element_type=jnp.float32
    )
    out_w_contract = scatter_sum(grad_w_contract.astype(jnp.bfloat16)).astype(jnp.float32)
    out_w_expand = scatter_sum(grad_w_expand.astype(jnp.bfloat16)).astype(jnp.float32)
    grad_b_expand = jnp.sum(grad_expanded.astype(jnp.float32), axis=0)
    grad_second = jnp.einsum(
        "tf,df->td", grad_expanded, w_expand, preferred_element_type=jnp.float32
    )
    grad_source_two, grad_gain_two, grad_shift_two = pull_two(grad_second)
    partial = (upstream.astype(jnp.float32) + grad_source_two).reshape(seqs, part_len, width)
    contracted = contracted.reshape(seqs, part_len, width)
    chain = ()
    sums = []
    for which in range(seqs):
        results = finish(
            which,
            returned[which],
            w_near,
            hidden_in,
            contracted,
            partial,
            gain_one[None],
            b_dense[None],
            tables,
            chain,
        )
        chain = results[:4]
        sums.append(results[4:])
    block_out, grad_input, grad_triple, context = chain
    grad_gain_one, grad_shift_one, grad_b_triple = (
        sum(each[1:], each[0])[0] for each in zip(*sums)
    )
    grad_w_triple = jnp.einsum(
        "td,te->de",
        low_one,
        grad_triple.reshape(tokens_here, 3 * width),
        preferred_element_type=jnp.float32,
    )
    grad_w_dense = jnp.einsum(
        "td,te->de",
        context.reshape(tokens_here, width),
        upstream,
        preferred_element_type=jnp.float32,
    )
    last = scatter_sum(
        jnp.concatenate(
            [grad_w_triple.astype(jnp.bfloat16), grad_w_dense.astype(jnp.bfloat16)], axis=1
        )
    ).astype(jnp.float32)
    out_w_triple = last[:, : 3 * width]
    out_w_dense = last[:, 3 * width :]
    totals = (
        grad_gain_one,
        grad_shift_one,
        grad_b_triple,
        upstream_total,
        grad_gain_two,
        grad_shift_two,
        grad_b_expand,
    )
    totals = [total.reshape(devices, -1) for total in totals]
    sizes = [total.shape[1] for total in totals]
    vector_grads = lax.psum_scatter(
        jnp.concatenate(totals, axis=1), axes, scatter_dimension=0, tiled=True
    ).reshape(-1)
    pieces = []
    offset = 0
    for size in sizes:
        pieces.append(vector_grads[offset : offset + size])
        offset += size
    out_gain_one, out_shift_one, out_b_triple, out_b_dense = pieces[:4]
    out_gain_two, out_shift_two, out_b_expand = pieces[4:]
    out_b_contract = out_b_dense
    return (
        block_out,
        grad_input,
        out_gain_one,
        out_shift_one,
        out_w_triple,
        out_b_triple,
        out_w_dense,
        out_b_dense,
        out_gain_two,
        out_shift_two,
        out_w_expand,
        out_b_expand,
        out_w_contract,
        out_b_contract,
    )


def solution(mesh):
    placed = (
        P("dp", "seq", None),
        P("dp", "seq", None),
        P(("dp", "seq")),
        P(("dp", "seq")),
        P(("dp", "seq"), None),
        P(("dp", "seq")),
        P(("dp", "seq"), None),
        P(("dp", "seq")),
        P(("dp", "seq")),
        P(("dp", "seq")),
        P(("dp", "seq"), None),
        P(("dp", "seq")),
        P(("dp", "seq"), None),
        P(("dp", "seq")),
    )
    return jax.shard_map(
        local,
        mesh=mesh,
        in_specs=placed,
        out_specs=(
            P("dp", "seq", None),
            P("dp", "seq", None),
            P(("dp", "seq")),
            P(("dp", "seq")),
            P(("dp", "seq"), None),
            P(("dp", "seq")),
            P(("dp", "seq"), None),
            P(("dp", "seq")),
            P(("dp", "seq")),
            P(("dp", "seq")),
            P(("dp", "seq"), None),
            P(("dp", "seq")),
            P(("dp", "seq"), None),
            P(("dp", "seq")),
        ),
        check_vma=False,
    )
```

```python
import math

import jax
import jax.numpy as jnp
from jax import lax
from jax.experimental import pallas as pl
from jax.experimental.pallas import tpu as pltpu
from jax.sharding import PartitionSpec as P

H = 16
HD = 64
ROT = 16


big_negative = -1e30
epsilon = 1e-05


def rotary_tables(positions, width):
    half = ROT // 2
    entry = jnp.arange(HD, dtype=jnp.int32)
    index = (entry % half).astype(jnp.float32)
    frequency = 10000.0 ** (-(index * 2.0 / ROT))
    angles = positions.astype(jnp.float32)[:, None] * frequency[None, :]
    cosine, sine = jnp.cos(angles), jnp.sin(angles)
    keep = jnp.where(entry < ROT, cosine, 1.0)
    ahead = jnp.where(entry < half, -sine, 0.0)
    behind = jnp.where((entry >= half) & (entry < ROT), sine, 0.0)
    return tuple(jnp.tile(table, (1, width // HD)) for table in (keep, ahead, behind))


def turn(values, keep, ahead, behind, sign):
    half = ROT // 2
    width = values.shape[-1]
    return values * keep + sign * (
        pltpu.roll(values, width - half, 1) * ahead + pltpu.roll(values, half, 1) * behind
    )


NT = (((1,), (1,)), ((), ()))


def normalize_body(x_ref, gain_one, shift_one, gain_two, shift_two, one_ref, two_ref, turned_ref):
    x = x_ref[...].astype(jnp.float32)
    average = jnp.mean(x, axis=-1, keepdims=True)
    centered = x - average
    scaled = centered * lax.rsqrt(jnp.mean(centered * centered, axis=-1, keepdims=True) + epsilon)
    one = scaled * gain_one[...] + shift_one[...]
    one_ref[...] = one.astype(jnp.bfloat16)
    two_ref[...] = (scaled * gain_two[...] + shift_two[...]).astype(jnp.bfloat16)
    turned_ref[...] = one.astype(jnp.bfloat16).T


def normalize(hidden, *rows):
    tokens, width = hidden.shape
    block = 256
    row = pl.BlockSpec((1, width), lambda i: (0, 0))
    here = pl.BlockSpec((block, width), lambda i: (i, 0))
    shape = jax.ShapeDtypeStruct((tokens, width), jnp.bfloat16)
    return pl.pallas_call(
        normalize_body,
        grid=(tokens // block,),
        in_specs=[here, row, row, row, row],
        out_specs=[here, here, pl.BlockSpec((width, block), lambda i: (0, i))],
        out_shape=[shape, shape, jax.ShapeDtypeStruct((width, tokens), jnp.bfloat16)],
        compiler_params=pltpu.CompilerParams(dimension_semantics=("arbitrary",)),
        cost_estimate=pl.CostEstimate(
            flops=10 * tokens * width, bytes_accessed=8 * tokens * width, transcendentals=0
        ),
        name="normalize",
    )(hidden, *rows)


def project_body(
    h_ref, y_ref, wq_ref, wk_ref, wv_ref, wd_ref, bq_ref, bk_ref, bv_ref, keep, ahead, behind, out_ref
):
    h = h_ref[...]
    for slot, w_ref, b_ref in ((0, wq_ref, bq_ref), (1, wk_ref, bk_ref)):
        t = jnp.dot(h, w_ref[...], preferred_element_type=jnp.float32) + b_ref[...]
        out_ref[slot] = turn(t, keep[...], ahead[...], behind[...], 1.0).astype(jnp.bfloat16)
    t = jnp.dot(h, wv_ref[...], preferred_element_type=jnp.float32) + bv_ref[...]
    out_ref[2] = t.astype(jnp.bfloat16)
    dc = lax.dot_general(y_ref[...], wd_ref[...], NT, preferred_element_type=jnp.float32)
    out_ref[3] = dc.astype(jnp.bfloat16)


def project(which, low_one, upstream, weights, bias, tables, part_len, groups):
    width = low_one.shape[1]
    mine = width // groups

    def columns(block):
        return pl.BlockSpec((width, mine), lambda g, b=block: (0, b * groups + g))

    def biases(block):
        return pl.BlockSpec((1, mine), lambda g, b=block: (0, b * groups + g))

    rows = pl.BlockSpec((part_len, width), lambda g: (which, 0))
    table = pl.BlockSpec((part_len, mine), lambda g: (0, 0))
    return pl.pallas_call(
        project_body,
        grid=(groups,),
        in_specs=[
            rows,
            rows,
            columns(0),
            columns(1),
            columns(2),
            pl.BlockSpec((mine, width), lambda g: (g, 3)),
            biases(0),
            biases(1),
            biases(2),
            table,
            table,
            table,
        ],
        out_specs=pl.BlockSpec((None, 4, part_len, mine), lambda g: (g, 0, 0, 0)),
        out_shape=jax.ShapeDtypeStruct((groups, 4, part_len, mine), jnp.bfloat16),
        compiler_params=pltpu.CompilerParams(
            dimension_semantics=("arbitrary",), vmem_limit_bytes=40 * 1024 * 1024
        ),
        cost_estimate=pl.CostEstimate(
            flops=part_len * width, bytes_accessed=part_len * width, transcendentals=0
        ),
        name="project",
    )(
        low_one,
        upstream,
        weights,
        weights,
        weights,
        weights,
        bias,
        bias,
        bias,
        *tables,
    )


def attention_body(
    heads, block, q_ref, k_ref, v_ref, dc_ref, out_ref, s_ref, dk_acc, dv_acc, kt_ref, vt_ref
):
    qi = pl.program_id(0)
    steps = pl.num_programs(0)
    scale = 1.0 / math.sqrt(HD)
    width = heads * HD

    @pl.when(qi == 0)
    def _():
        dk_acc[...] = jnp.zeros_like(dk_acc)
        dv_acc[...] = jnp.zeros_like(dv_acc)

        @pl.loop(0, steps)
        def _(ki):
            kt_ref[ki] = k_ref[ki].T
            vt_ref[ki] = v_ref[ki].T

    lane = lax.broadcasted_iota(jnp.int32, (block, width), 1) // HD
    causal = lax.broadcasted_iota(jnp.int32, (block, block), 0) <= lax.broadcasted_iota(
        jnp.int32, (block, block), 1
    )
    q_all = q_ref[...] * jnp.bfloat16(scale)
    dc_all = dc_ref[...]
    contexts = []
    grads = []
    for h in range(heads):
        zero = jnp.zeros_like(q_all)
        q = jnp.where(lane == h, q_all, zero)
        dc = jnp.where(lane == h, dc_all, zero)
        rows = pl.ds(h * HD, HD)

        def scores(ki, q=q):
            return lax.dot_general(k_ref[ki], q, NT, preferred_element_type=jnp.float32)

        def first(ki, highest, scores=scores):
            s = scores(ki)
            s_ref[ki] = s
            return jnp.maximum(highest, jnp.max(s, axis=0, keepdims=True))

        diagonal = jnp.where(causal, scores(qi), big_negative)
        s_ref[qi] = diagonal
        highest = lax.fori_loop(0, qi, first, jnp.max(diagonal, axis=0, keepdims=True))

        def second(ki, carry, highest=highest, rows=rows):
            total, context = carry
            e = jnp.exp(s_ref[ki] - highest)
            total = total + jnp.sum(e, axis=0, keepdims=True)
            context = context + jnp.dot(
                vt_ref[ki, rows, :], e.astype(jnp.bfloat16), preferred_element_type=jnp.float32
            )
            return (total, context)

        total, context = lax.fori_loop(
            0,
            qi + 1,
            second,
            (jnp.zeros((1, block), jnp.float32), jnp.zeros((HD, block), jnp.float32)),
        )
        context = context / total
        log_total = highest + jnp.log(total)
        contexts.append(context)
        dct = dc_all[:, h * HD : (h + 1) * HD].astype(jnp.float32).T
        inner = jnp.sum(context * dct, axis=0, keepdims=True)

        def third(ki, grad, q=q, dc=dc, inner=inner, log_total=log_total, rows=rows):
            p = jnp.exp(s_ref[ki] - log_total)
            dp = lax.dot_general(v_ref[ki], dc, NT, preferred_element_type=jnp.float32)
            ds = (p * (dp - inner)).astype(jnp.bfloat16)
            dv_acc[ki] += jnp.dot(p.astype(jnp.bfloat16), dc, preferred_element_type=jnp.float32)
            dk_acc[ki] += jnp.dot(ds, q, preferred_element_type=jnp.float32)
            return grad + jnp.dot(kt_ref[ki, rows, :], ds, preferred_element_type=jnp.float32)

        grad = lax.fori_loop(0, qi + 1, third, jnp.zeros((HD, block), jnp.float32))
        grads.append(grad * scale)
    out_ref[qi, 0] = jnp.concatenate(contexts, axis=0).T.astype(jnp.bfloat16)
    out_ref[qi, 1] = jnp.concatenate(grads, axis=0).T.astype(jnp.bfloat16)

    @pl.when(qi == steps - 1)
    def _():
        @pl.loop(0, steps)
        def _(ki):
            out_ref[ki, 2] = dk_acc[ki].astype(jnp.bfloat16)
            out_ref[ki, 3] = dv_acc[ki].astype(jnp.bfloat16)


def attention(parts):
    groups, _, block, width = parts.shape
    heads = width // HD
    length = groups * block

    def rows_of(which):
        return pl.BlockSpec((None, None, block, width), lambda i, w=which: (i, w, 0, 0))

    def whole_of(which):
        return pl.BlockSpec((groups, None, block, width), lambda i, w=which: (0, w, 0, 0))

    def body(*refs):
        attention_body(heads, block, *refs)

    return pl.pallas_call(
        body,
        grid=(groups,),
        in_specs=[rows_of(0), whole_of(1), whole_of(2), rows_of(3)],
        out_specs=pl.BlockSpec(parts.shape, lambda i: (0, 0, 0, 0)),
        out_shape=jax.ShapeDtypeStruct(parts.shape, jnp.bfloat16),
        scratch_shapes=[
            pltpu.VMEM((groups, block, block), jnp.float32),
            pltpu.VMEM((groups, block, width), jnp.float32),
            pltpu.VMEM((groups, block, width), jnp.float32),
            pltpu.VMEM((groups, width, block), jnp.bfloat16),
            pltpu.VMEM((groups, width, block), jnp.bfloat16),
        ],
        compiler_params=pltpu.CompilerParams(
            dimension_semantics=("arbitrary",), vmem_limit_bytes=50 * 1024 * 1024
        ),
        cost_estimate=pl.CostEstimate(
            flops=length * width, bytes_accessed=length * width, transcendentals=0
        ),
        name="attention",
    )(parts, parts, parts, parts)


def finish_body(
    groups,
    mine,
    chained,
    r_ref,
    w_ref,
    x_ref,
    y_ref,
    f_ref,
    second_ref,
    gain_ref,
    gain_two_ref,
    bias_ref,
    keep,
    ahead,
    behind,
    *refs,
):
    out_ref, grad_ref, dt_ref, c_ref, gain_sum, shift_sum, bias_sum = refs[chained : chained + 7]
    gain_two_sum, shift_two_sum = refs[chained + 7 :]
    width = groups * mine

    @pl.when(pl.program_id(0) == 0)
    def _():
        gain_sum[...] = jnp.zeros_like(gain_sum)
        shift_sum[...] = jnp.zeros_like(shift_sum)
        bias_sum[...] = jnp.zeros_like(bias_sum)
        gain_two_sum[...] = jnp.zeros_like(gain_two_sum)
        shift_two_sum[...] = jnp.zeros_like(shift_two_sum)

    x = x_ref[...].astype(jnp.float32)
    for g in range(groups):
        at = g * mine
        for slot in (1, 2):
            turned = turn(
                r_ref[g, slot].astype(jnp.float32), keep[...], ahead[...], behind[...], -1.0
            ).astype(jnp.bfloat16)
            here = (slot - 1) * width + at
            dt_ref[:, here : here + mine] = turned
        dt_ref[:, 2 * width + at : 2 * width + at + mine] = r_ref[g, 3]
    context = jnp.concatenate([r_ref[g, 0] for g in range(groups)], axis=1)
    c_ref[...] = context.T
    attended = jnp.dot(
        context, w_ref[:, 3 * width : 4 * width], preferred_element_type=jnp.float32
    )
    out_ref[...] = (x + (attended + bias_ref[...]) + f_ref[...]).astype(jnp.bfloat16)
    dt = dt_ref[...]
    bias_sum[...] += jnp.sum(dt.astype(jnp.float32), axis=0, keepdims=True)
    dh = lax.dot_general(dt, w_ref[:, : 3 * width], NT, preferred_element_type=jnp.float32)
    average = jnp.mean(x, axis=-1, keepdims=True)
    centered = x - average
    inverse = lax.rsqrt(jnp.mean(centered * centered, axis=-1, keepdims=True) + epsilon)
    xh = centered * inverse
    gain_sum[...] += jnp.sum(dh * xh, axis=0, keepdims=True)
    shift_sum[...] += jnp.sum(dh, axis=0, keepdims=True)
    dh_two = second_ref[...]
    gain_two_sum[...] += jnp.sum(dh_two * xh, axis=0, keepdims=True)
    shift_two_sum[...] += jnp.sum(dh_two, axis=0, keepdims=True)
    dg = dh * gain_ref[...] + dh_two * gain_two_ref[...]
    first = jnp.mean(dg, axis=-1, keepdims=True)
    second = jnp.mean(dg * xh, axis=-1, keepdims=True)
    grad_ref[...] = y_ref[...].astype(jnp.float32) + (dg - first - xh * second) * inverse


def finish(
    which, returned, weights, hidden, upstream, contracted, second, gains, bias, tables, chain
):
    groups, _, part_len, mine = returned.shape
    seqs, _, width = hidden.shape
    block = min(256, part_len)
    chain = tuple(chain)

    def row(size):
        return pl.BlockSpec((1, size), lambda j: (0, 0))

    tokens = pl.BlockSpec((None, block, width), lambda j: (which, j, 0))
    triple = pl.BlockSpec((block, 3 * width), lambda j: (j, 0))
    turned = pl.BlockSpec((width, block), lambda j: (0, j))
    table = pl.BlockSpec((block, mine), lambda j: (j, 0))
    ordinary = 12

    def body(*refs):
        finish_body(groups, mine, len(chain), *refs)

    return pl.pallas_call(
        body,
        grid=(part_len // block,),
        in_specs=[
            pl.BlockSpec((groups, 4, block, mine), lambda j: (0, 0, j, 0)),
            pl.BlockSpec(weights.shape, lambda j: (0, 0)),
            tokens,
            tokens,
            tokens,
            tokens,
            row(width),
            row(width),
            row(width),
            table,
            table,
            table,
        ]
        + [pl.BlockSpec(memory_space=pl.ANY)] * len(chain),
        out_specs=[tokens, tokens, triple, turned, row(width), row(width), row(3 * width)]
        + [row(width), row(width)],
        out_shape=[
            jax.ShapeDtypeStruct((seqs, part_len, width), jnp.bfloat16),
            jax.ShapeDtypeStruct((seqs, part_len, width), jnp.float32),
            jax.ShapeDtypeStruct((part_len, 3 * width), jnp.bfloat16),
            jax.ShapeDtypeStruct((width, part_len), jnp.bfloat16),
            jax.ShapeDtypeStruct((1, width), jnp.float32),
            jax.ShapeDtypeStruct((1, width), jnp.float32),
            jax.ShapeDtypeStruct((1, 3 * width), jnp.float32),
            jax.ShapeDtypeStruct((1, width), jnp.float32),
            jax.ShapeDtypeStruct((1, width), jnp.float32),
        ],
        input_output_aliases={ordinary + i: i for i in range(len(chain))},
        compiler_params=pltpu.CompilerParams(
            dimension_semantics=("arbitrary",), vmem_limit_bytes=56 * 1024 * 1024
        ),
        cost_estimate=pl.CostEstimate(
            flops=part_len * width, bytes_accessed=part_len * width, transcendentals=0
        ),
        name="finish",
    )(
        returned, weights, hidden, upstream, contracted, second, *gains, bias, *tables, *chain
    )


def product(low_ref, grad_refs, context_refs, y_ref, tiles):
    step = pl.program_id(0)
    part_len = grad_refs[0].shape[0]

    def triple():
        return sum(
            jnp.dot(
                low_ref[:, i * part_len : (i + 1) * part_len],
                grad_ref[...],
                preferred_element_type=jnp.float32,
            )
            for i, grad_ref in enumerate(grad_refs)
        )

    def dense():
        return sum(
            jnp.dot(
                context_ref[...],
                y_ref[i * part_len : (i + 1) * part_len, :],
                preferred_element_type=jnp.float32,
            )
            for i, context_ref in enumerate(context_refs)
        )

    return step < 3 * tiles, triple, (step >= 3 * tiles) & (step < 4 * tiles), dense


def early_gradient_body(tiles, count, low_ref, y_ref, *refs):
    out_ref = refs[-1]
    is_triple, triple, is_dense, dense = product(
        low_ref, refs[:count], refs[count : 2 * count], y_ref, tiles
    )

    @pl.when(is_triple)
    def _():
        out_ref[...] = triple()

    @pl.when(is_dense)
    def _():
        out_ref[...] = dense()


def late_gradient_body(
    tiles, devices, low_ref, y_ref, grad_ref, context_ref, early_ref, *refs
):
    out_ref = refs[-1]
    vector_refs = refs[:-1]
    is_triple, triple, is_dense, dense = product(
        low_ref, [grad_ref], [context_ref], y_ref, tiles
    )

    @pl.when(is_triple)
    def _():
        out_ref[...] = (early_ref[...] + triple()).astype(jnp.bfloat16)

    @pl.when(is_dense)
    def _():
        out_ref[...] = (early_ref[...] + dense()).astype(jnp.bfloat16)

    @pl.when(pl.program_id(0) == 4 * tiles)
    def _():
        shard = out_ref.shape[0] // devices
        per = (len(vector_refs) - 2) // 5
        sums = [
            sum(ref[...] for ref in vector_refs[i * per : (i + 1) * per]) for i in range(5)
        ]
        sums += [ref[...] for ref in vector_refs[-2:]]
        blank = jnp.zeros((shard, 128), jnp.float32)
        place = lax.broadcasted_iota(jnp.int32, (shard, 128), 0)
        for device in range(devices):
            block = blank
            for row, members in enumerate(ROWS):
                pieces = []
                for at in members:
                    size = sums[at].shape[1] // devices
                    pieces.append(sums[at][:, device * size : (device + 1) * size])
                wide = sum(piece.shape[1] for piece in pieces)
                if wide < 128:
                    pieces.append(jnp.zeros((1, 128 - wide), jnp.float32))
                line = jnp.concatenate(pieces, axis=1)
                block = jnp.where(place == row, line, block)
            out_ref[device * shard : (device + 1) * shard, :128] = block.astype(jnp.bfloat16)


ROWS = ((0, 1, 3, 4), (5,), (2,), (6,))


def early_gradient(turned, upstream, grads, contexts):
    width = turned.shape[0]
    count = len(grads)
    part_len = grads[0].shape[0]
    tokens = count * part_len
    tile = 256
    tiles = width // tile

    def body(*refs):
        early_gradient_body(tiles, count, *refs)

    return pl.pallas_call(
        body,
        grid=(4 * tiles,),
        in_specs=[
            pl.BlockSpec((width, tokens), lambda n: (0, 0)),
            pl.BlockSpec((tokens, tile), lambda n: (0, jnp.clip(n - 3 * tiles, 0, tiles - 1))),
        ]
        + [pl.BlockSpec((part_len, tile), lambda n: (0, jnp.minimum(n, 3 * tiles - 1)))] * count
        + [pl.BlockSpec((width, part_len), lambda n: (0, 0))] * count,
        out_specs=pl.BlockSpec((width, tile), lambda n: (0, n)),
        out_shape=jax.ShapeDtypeStruct((width, 4 * width), jnp.float32),
        compiler_params=pltpu.CompilerParams(
            dimension_semantics=("arbitrary",), vmem_limit_bytes=40 * 1024 * 1024
        ),
        cost_estimate=pl.CostEstimate(
            flops=part_len * width, bytes_accessed=part_len * width, transcendentals=0
        ),
        name="early_gradient",
    )(turned, upstream, *grads, *contexts)


def late_gradient(devices, turned, upstream, grad, context, early, vectors):
    width = turned.shape[0]
    part_len = grad.shape[0]
    last = turned.shape[1] // part_len - 1
    tile = 256
    tiles = width // tile

    def body(*refs):
        late_gradient_body(tiles, devices, *refs)

    return pl.pallas_call(
        body,
        grid=(4 * tiles + 1,),
        in_specs=[
            pl.BlockSpec((width, part_len), lambda n: (0, last)),
            pl.BlockSpec(
                (part_len, tile), lambda n: (last, jnp.clip(n - 3 * tiles, 0, tiles - 1))
            ),
            pl.BlockSpec((part_len, tile), lambda n: (0, jnp.minimum(n, 3 * tiles - 1))),
            pl.BlockSpec((width, part_len), lambda n: (0, 0)),
            pl.BlockSpec((width, tile), lambda n: (0, jnp.minimum(n, 4 * tiles - 1))),
        ]
        + [pl.BlockSpec(vector.shape, lambda n: (0, 0)) for vector in vectors],
        out_specs=pl.BlockSpec((width, tile), lambda n: (0, n)),
        out_shape=jax.ShapeDtypeStruct((width, 4 * width + 128), jnp.bfloat16),
        compiler_params=pltpu.CompilerParams(
            dimension_semantics=("arbitrary",), vmem_limit_bytes=40 * 1024 * 1024
        ),
        cost_estimate=pl.CostEstimate(
            flops=2 * width * width * part_len,
            bytes_accessed=24 * width * width,
            transcendentals=0,
        ),
        name="late_gradient",
    )(turned, upstream, grad, context, early, *vectors)


def after(value, *others):
    return lax.optimization_barrier((value, *others))[0]


def scatter_sum(values):
    return lax.psum_scatter(values, "dp", scatter_dimension=0, tiled=True)


def local(
    hidden_in,
    cotangent,
    first_gain,
    first_shift,
    triple_weight,
    triple_bias,
    dense_weight,
    dense_bias,
    second_gain,
    second_shift,
    expand_weight,
    expand_bias,
    contract_weight,
    contract_bias,
):
    axes = ("dp", "seq")
    devices = lax.axis_size("dp") * lax.axis_size("seq")
    groups = lax.axis_size("seq")
    seqs, part_len, width = hidden_in.shape
    tokens_here = seqs * part_len
    shard = triple_weight.shape[0]
    vectors = (
        first_gain,
        first_shift,
        triple_bias,
        dense_bias,
        second_gain,
        second_shift,
        expand_bias,
        contract_bias,
    )
    columns = [vector.reshape(shard, -1) for vector in vectors]
    used = sum(column.shape[1] for column in columns)
    padding = jnp.zeros((shard, 128 - used), jnp.bfloat16)
    w_near = lax.all_gather(
        jnp.concatenate([triple_weight, dense_weight, *columns, padding], axis=1),
        axes,
        axis=0,
        tiled=True,
    )
    stacked = w_near[:, 4 * width : 4 * width + used].astype(jnp.float32)
    whole = []
    offset = 0
    for column in columns:
        size = column.shape[1]
        whole.append(stacked[:, offset : offset + size].reshape(-1))
        offset += size
    gain_one, shift_one, b_triple, b_dense, gain_two, shift_two, b_expand, b_contract = whole
    far = jnp.concatenate([expand_weight, contract_weight.reshape(shard, -1)], axis=1)
    hidden = expand_weight.shape[1]
    far = lax.all_gather(after(far, w_near), "seq", axis=0, tiled=True)
    upstream = cotangent.reshape(tokens_here, width)
    low_one, low_two, turned_one = normalize(
        hidden_in.reshape(tokens_here, width),
        gain_one[None],
        shift_one[None],
        gain_two[None],
        shift_two[None],
    )
    positions = lax.axis_index("seq") * part_len + jnp.arange(part_len, dtype=jnp.int32)
    tables = rotary_tables(positions, width // groups)
    sent = [
        project(which, low_one, upstream, w_near, b_triple[None], tables, part_len, groups)
        for which in range(seqs)
    ]

    def exchange(values):
        return lax.all_to_all(values, "seq", split_axis=0, concat_axis=0, tiled=True)

    received_0 = exchange(sent[0])
    received_1 = exchange(sent[1])
    far = after(far, sent[0])
    w_expand = lax.all_gather(far[:, :hidden], "dp", axis=0, tiled=True)
    w_contract = lax.all_gather(far[:, hidden:].reshape(-1, width), "dp", axis=0, tiled=True)
    low_two = after(low_two, received_0, *sent)
    expanded = jnp.dot(low_two, w_expand, preferred_element_type=jnp.float32) + b_expand
    activated, pull_gelu = jax.vjp(lambda inner: jax.nn.gelu(inner, approximate=False), expanded)
    low_act = activated.astype(jnp.bfloat16)
    received_2 = exchange(after(sent[2], low_act))
    outcome_0 = attention(after(received_0, received_1, low_act))
    upstream_ffn = after(upstream, outcome_0)
    grad_act = jnp.einsum(
        "td,fd->tf", upstream_ffn, w_contract, preferred_element_type=jnp.float32
    )
    grad_expanded = pull_gelu(grad_act)[0].astype(jnp.bfloat16)
    grad_b_expand = jnp.sum(grad_expanded.astype(jnp.float32), axis=0)
    outcome_1 = attention(after(received_1, received_2, grad_expanded))
    returned_0 = exchange(after(outcome_0, grad_expanded))
    grad_w_contract = jnp.einsum(
        "tf,td->fd", after(low_act, outcome_1), upstream, preferred_element_type=jnp.float32
    ).astype(jnp.bfloat16)
    outcome_2 = attention(after(received_2, returned_0, grad_w_contract))
    returned_1 = exchange(after(outcome_1, grad_w_contract))
    grad_w_expand = jnp.einsum(
        "td,tf->df",
        low_two,
        after(grad_expanded, outcome_2),
        preferred_element_type=jnp.float32,
    ).astype(jnp.bfloat16)
    returned_2 = exchange(after(outcome_2, grad_w_expand))
    sum_w_contract = scatter_sum(after(grad_w_contract, returned_0))
    sum_w_expand = scatter_sum(after(grad_w_expand, returned_1))
    grad_second = jnp.einsum(
        "tf,df->td", after(grad_expanded, returned_1), w_expand, preferred_element_type=jnp.float32
    )
    grad_second = grad_second.reshape(seqs, part_len, width)
    contracted = (
        jnp.dot(after(low_act, returned_1), w_contract, preferred_element_type=jnp.float32)
        + b_contract
    )
    upstream_total = jnp.sum(upstream.astype(jnp.float32), axis=0)
    contracted = contracted.reshape(seqs, part_len, width)
    returned = [returned_0, returned_1, returned_2]
    chain = ()
    grads = []
    contexts = []
    sums = []
    for which in range(seqs):
        if which == seqs - 1:
            early = early_gradient(turned_one, upstream, grads, contexts)
        results = finish(
            which,
            returned[which],
            w_near,
            hidden_in,
            cotangent,
            contracted,
            grad_second,
            (gain_one[None], gain_two[None]),
            b_dense[None],
            tables,
            chain,
        )
        chain = results[:2]
        grads.append(results[2])
        contexts.append(results[3])
        sums.append(results[4:])
    block_out, grad_input = chain
    vectors = [each for group in zip(*sums) for each in group]
    vectors += [upstream_total[None], grad_b_expand[None]]
    near = late_gradient(
        devices, turned_one, upstream, grads[-1], contexts[-1], early, vectors
    )
    near = scatter_sum(near)
    last = lax.psum_scatter(near, "seq", scatter_dimension=0, tiled=True).astype(jnp.float32)
    rows_here = near.shape[0]
    far = jnp.concatenate([sum_w_expand, sum_w_contract.reshape(rows_here, -1)], axis=1)
    far = lax.all_to_all(
        far.reshape(groups, -1, far.shape[1]), "seq", split_axis=0, concat_axis=0, tiled=True
    )
    out_w_expand = jnp.sum(far[:, :, :hidden].astype(jnp.float32), axis=0)
    out_w_contract = jnp.sum(far[:, :, hidden:].astype(jnp.float32), axis=0).reshape(-1, width)
    out_w_triple = last[:, : 3 * width]
    out_w_dense = last[:, 3 * width : 4 * width]
    small = last[:, 4 * width : 4 * width + 128]
    sizes = [vector.shape[1] // devices for vector in vectors[:-2:seqs] + vectors[-2:]]
    pieces = [None] * len(sizes)
    for row, members in enumerate(ROWS):
        offset = 0
        for at in members:
            pieces[at] = small[row, offset : offset + sizes[at]]
            offset += sizes[at]
    out_gain_one, out_shift_one, out_b_triple, out_gain_two, out_shift_two = pieces[:5]
    out_b_dense, out_b_expand = pieces[5:]
    out_b_contract = out_b_dense
    return (
        block_out,
        grad_input,
        out_gain_one,
        out_shift_one,
        out_w_triple,
        out_b_triple,
        out_w_dense,
        out_b_dense,
        out_gain_two,
        out_shift_two,
        out_w_expand,
        out_b_expand,
        out_w_contract,
        out_b_contract,
    )


def solution(mesh):
    placed = (
        P("dp", "seq", None),
        P("dp", "seq", None),
        P(("dp", "seq")),
        P(("dp", "seq")),
        P(("dp", "seq"), None),
        P(("dp", "seq")),
        P(("dp", "seq"), None),
        P(("dp", "seq")),
        P(("dp", "seq")),
        P(("dp", "seq")),
        P(("dp", "seq"), None),
        P(("dp", "seq")),
        P(("dp", "seq"), None),
        P(("dp", "seq")),
    )
    return jax.shard_map(
        local,
        mesh=mesh,
        in_specs=placed,
        out_specs=(
            P("dp", "seq", None),
            P("dp", "seq", None),
            P(("dp", "seq")),
            P(("dp", "seq")),
            P(("dp", "seq"), None),
            P(("dp", "seq")),
            P(("dp", "seq"), None),
            P(("dp", "seq")),
            P(("dp", "seq")),
            P(("dp", "seq")),
            P(("dp", "seq"), None),
            P(("dp", "seq")),
            P(("dp", "seq"), None),
            P(("dp", "seq")),
        ),
        check_vma=False,
    )
```

```python
import math

import jax
import jax.numpy as jnp
from jax import lax
from jax.experimental import pallas as pl
from jax.experimental.pallas import tpu as pltpu
from jax.sharding import PartitionSpec as P

H = 16
HD = 64
ROT = 16


big_negative = -1e30
epsilon = 1e-05


def rotary_tables(positions, width):
    half = ROT // 2
    entry = jnp.arange(HD, dtype=jnp.int32)
    index = (entry % half).astype(jnp.float32)
    frequency = 10000.0 ** (-(index * 2.0 / ROT))
    angles = positions.astype(jnp.float32)[:, None] * frequency[None, :]
    cosine, sine = jnp.cos(angles), jnp.sin(angles)
    keep = jnp.where(entry < ROT, cosine, 1.0)
    ahead = jnp.where(entry < half, -sine, 0.0)
    behind = jnp.where((entry >= half) & (entry < ROT), sine, 0.0)
    return tuple(jnp.tile(table, (1, width // HD)) for table in (keep, ahead, behind))


def turn(values, keep, ahead, behind, sign):
    half = ROT // 2
    width = values.shape[-1]
    return values * keep + sign * (
        pltpu.roll(values, width - half, 1) * ahead + pltpu.roll(values, half, 1) * behind
    )


NT = (((1,), (1,)), ((), ()))


def normalize_body(x_ref, gain_one, shift_one, gain_two, shift_two, one_ref, two_ref, turned_ref):
    x = x_ref[...].astype(jnp.float32)
    average = jnp.mean(x, axis=-1, keepdims=True)
    centered = x - average
    scaled = centered * lax.rsqrt(jnp.mean(centered * centered, axis=-1, keepdims=True) + epsilon)
    one = scaled * gain_one[...] + shift_one[...]
    one_ref[...] = one.astype(jnp.bfloat16)
    two_ref[...] = (scaled * gain_two[...] + shift_two[...]).astype(jnp.bfloat16)
    turned_ref[...] = one.astype(jnp.bfloat16).T


def normalize(hidden, *rows):
    tokens, width = hidden.shape
    block = 256
    row = pl.BlockSpec((1, width), lambda i: (0, 0))
    here = pl.BlockSpec((block, width), lambda i: (i, 0))
    shape = jax.ShapeDtypeStruct((tokens, width), jnp.bfloat16)
    return pl.pallas_call(
        normalize_body,
        grid=(tokens // block,),
        in_specs=[here, row, row, row, row],
        out_specs=[here, here, pl.BlockSpec((width, block), lambda i: (0, i))],
        out_shape=[shape, shape, jax.ShapeDtypeStruct((width, tokens), jnp.bfloat16)],
        compiler_params=pltpu.CompilerParams(dimension_semantics=("arbitrary",)),
        cost_estimate=pl.CostEstimate(
            flops=10 * tokens * width, bytes_accessed=8 * tokens * width, transcendentals=0
        ),
        name="normalize",
    )(hidden, *rows)


def project_body(
    h_ref, y_ref, wq_ref, wk_ref, wv_ref, wd_ref, bq_ref, bk_ref, bv_ref, keep, ahead, behind, out_ref
):
    h = h_ref[...]
    for slot, w_ref, b_ref in ((0, wq_ref, bq_ref), (1, wk_ref, bk_ref)):
        t = jnp.dot(h, w_ref[...], preferred_element_type=jnp.float32) + b_ref[...]
        out_ref[slot] = turn(t, keep[...], ahead[...], behind[...], 1.0).astype(jnp.bfloat16)
    t = jnp.dot(h, wv_ref[...], preferred_element_type=jnp.float32) + bv_ref[...]
    out_ref[2] = t.astype(jnp.bfloat16)
    dc = lax.dot_general(y_ref[...], wd_ref[...], NT, preferred_element_type=jnp.float32)
    out_ref[3] = dc.astype(jnp.bfloat16)


def project(which, low_one, upstream, weights, bias, tables, part_len, groups):
    width = low_one.shape[1]
    mine = width // groups

    def columns(block):
        return pl.BlockSpec((width, mine), lambda g, b=block: (0, b * groups + g))

    def biases(block):
        return pl.BlockSpec((1, mine), lambda g, b=block: (0, b * groups + g))

    rows = pl.BlockSpec((part_len, width), lambda g: (which, 0))
    table = pl.BlockSpec((part_len, mine), lambda g: (0, 0))
    return pl.pallas_call(
        project_body,
        grid=(groups,),
        in_specs=[
            rows,
            rows,
            columns(0),
            columns(1),
            columns(2),
            pl.BlockSpec((mine, width), lambda g: (g, 3)),
            biases(0),
            biases(1),
            biases(2),
            table,
            table,
            table,
        ],
        out_specs=pl.BlockSpec((None, 4, part_len, mine), lambda g: (g, 0, 0, 0)),
        out_shape=jax.ShapeDtypeStruct((groups, 4, part_len, mine), jnp.bfloat16),
        compiler_params=pltpu.CompilerParams(
            dimension_semantics=("arbitrary",), vmem_limit_bytes=40 * 1024 * 1024
        ),
        cost_estimate=pl.CostEstimate(
            flops=part_len * width, bytes_accessed=part_len * width, transcendentals=0
        ),
        name="project",
    )(
        low_one,
        upstream,
        weights,
        weights,
        weights,
        weights,
        bias,
        bias,
        bias,
        *tables,
    )


def attention_body(
    heads, block, q_ref, k_ref, v_ref, dc_ref, out_ref, s_ref, dk_acc, dv_acc, kt_ref, vt_ref
):
    qi = pl.program_id(0)
    steps = pl.num_programs(0)
    scale = 1.0 / math.sqrt(HD)
    width = heads * HD

    @pl.when(qi == 0)
    def _():
        dk_acc[...] = jnp.zeros_like(dk_acc)
        dv_acc[...] = jnp.zeros_like(dv_acc)

        @pl.loop(0, steps)
        def _(ki):
            kt_ref[ki] = k_ref[ki].T
            vt_ref[ki] = v_ref[ki].T

    lane = lax.broadcasted_iota(jnp.int32, (block, width), 1) // HD
    causal = lax.broadcasted_iota(jnp.int32, (block, block), 0) <= lax.broadcasted_iota(
        jnp.int32, (block, block), 1
    )
    q_all = q_ref[...] * jnp.bfloat16(scale)
    dc_all = dc_ref[...]
    contexts = []
    grads = []
    for h in range(heads):
        zero = jnp.zeros_like(q_all)
        q = jnp.where(lane == h, q_all, zero)
        dc = jnp.where(lane == h, dc_all, zero)
        rows = pl.ds(h * HD, HD)

        def scores(ki, q=q):
            return lax.dot_general(k_ref[ki], q, NT, preferred_element_type=jnp.float32)

        def first(ki, highest, scores=scores):
            s = scores(ki)
            s_ref[ki] = s
            return jnp.maximum(highest, jnp.max(s, axis=0, keepdims=True))

        diagonal = jnp.where(causal, scores(qi), big_negative)
        s_ref[qi] = diagonal
        highest = lax.fori_loop(0, qi, first, jnp.max(diagonal, axis=0, keepdims=True))

        def second(ki, carry, highest=highest, rows=rows):
            total, context = carry
            e = jnp.exp(s_ref[ki] - highest)
            total = total + jnp.sum(e, axis=0, keepdims=True)
            context = context + jnp.dot(
                vt_ref[ki, rows, :], e.astype(jnp.bfloat16), preferred_element_type=jnp.float32
            )
            return (total, context)

        total, context = lax.fori_loop(
            0,
            qi + 1,
            second,
            (jnp.zeros((1, block), jnp.float32), jnp.zeros((HD, block), jnp.float32)),
        )
        context = context / total
        log_total = highest + jnp.log(total)
        contexts.append(context)
        dct = dc_all[:, h * HD : (h + 1) * HD].astype(jnp.float32).T
        inner = jnp.sum(context * dct, axis=0, keepdims=True)

        def third(ki, grad, q=q, dc=dc, inner=inner, log_total=log_total, rows=rows):
            p = jnp.exp(s_ref[ki] - log_total)
            dp = lax.dot_general(v_ref[ki], dc, NT, preferred_element_type=jnp.float32)
            ds = (p * (dp - inner)).astype(jnp.bfloat16)
            dv_acc[ki] += jnp.dot(p.astype(jnp.bfloat16), dc, preferred_element_type=jnp.float32)
            dk_acc[ki] += jnp.dot(ds, q, preferred_element_type=jnp.float32)
            return grad + jnp.dot(kt_ref[ki, rows, :], ds, preferred_element_type=jnp.float32)

        grad = lax.fori_loop(0, qi + 1, third, jnp.zeros((HD, block), jnp.float32))
        grads.append(grad * scale)
    out_ref[qi, 0] = jnp.concatenate(contexts, axis=0).T.astype(jnp.bfloat16)
    out_ref[qi, 1] = jnp.concatenate(grads, axis=0).T.astype(jnp.bfloat16)

    @pl.when(qi == steps - 1)
    def _():
        @pl.loop(0, steps)
        def _(ki):
            out_ref[ki, 2] = dk_acc[ki].astype(jnp.bfloat16)
            out_ref[ki, 3] = dv_acc[ki].astype(jnp.bfloat16)


def attention(parts):
    groups, _, block, width = parts.shape
    heads = width // HD
    length = groups * block

    def rows_of(which):
        return pl.BlockSpec((None, None, block, width), lambda i, w=which: (i, w, 0, 0))

    def whole_of(which):
        return pl.BlockSpec((groups, None, block, width), lambda i, w=which: (0, w, 0, 0))

    def body(*refs):
        attention_body(heads, block, *refs)

    return pl.pallas_call(
        body,
        grid=(groups,),
        in_specs=[rows_of(0), whole_of(1), whole_of(2), rows_of(3)],
        out_specs=pl.BlockSpec(parts.shape, lambda i: (0, 0, 0, 0)),
        out_shape=jax.ShapeDtypeStruct(parts.shape, jnp.bfloat16),
        scratch_shapes=[
            pltpu.VMEM((groups, block, block), jnp.float32),
            pltpu.VMEM((groups, block, width), jnp.float32),
            pltpu.VMEM((groups, block, width), jnp.float32),
            pltpu.VMEM((groups, width, block), jnp.bfloat16),
            pltpu.VMEM((groups, width, block), jnp.bfloat16),
        ],
        compiler_params=pltpu.CompilerParams(
            dimension_semantics=("arbitrary",), vmem_limit_bytes=50 * 1024 * 1024
        ),
        cost_estimate=pl.CostEstimate(
            flops=length * width, bytes_accessed=length * width, transcendentals=0
        ),
        name="attention",
    )(parts, parts, parts, parts)


def unrotate_body(groups, mine, r_ref, keep, ahead, behind, dt_ref, c_ref, bias_sum):
    width = groups * mine

    @pl.when(pl.program_id(0) == 0)
    def _():
        bias_sum[...] = jnp.zeros_like(bias_sum)

    for g in range(groups):
        at = g * mine
        for slot in (1, 2):
            turned = turn(
                r_ref[g, slot].astype(jnp.float32), keep[...], ahead[...], behind[...], -1.0
            ).astype(jnp.bfloat16)
            here = (slot - 1) * width + at
            dt_ref[:, here : here + mine] = turned
        dt_ref[:, 2 * width + at : 2 * width + at + mine] = r_ref[g, 3]
        c_ref[at : at + mine, :] = r_ref[g, 0].T
    bias_sum[...] += jnp.sum(dt_ref[...].astype(jnp.float32), axis=0, keepdims=True)


def unrotate(returned, tables):
    groups, _, part_len, mine = returned.shape
    width = groups * mine
    block = min(256, part_len)

    def body(*refs):
        unrotate_body(groups, mine, *refs)

    return pl.pallas_call(
        body,
        grid=(part_len // block,),
        in_specs=[pl.BlockSpec((groups, 4, block, mine), lambda j: (0, 0, j, 0))]
        + [pl.BlockSpec((block, mine), lambda j: (j, 0))] * 3,
        out_specs=[
            pl.BlockSpec((block, 3 * width), lambda j: (j, 0)),
            pl.BlockSpec((width, block), lambda j: (0, j)),
            pl.BlockSpec((1, 3 * width), lambda j: (0, 0)),
        ],
        out_shape=[
            jax.ShapeDtypeStruct((part_len, 3 * width), jnp.bfloat16),
            jax.ShapeDtypeStruct((width, part_len), jnp.bfloat16),
            jax.ShapeDtypeStruct((1, 3 * width), jnp.float32),
        ],
        compiler_params=pltpu.CompilerParams(
            dimension_semantics=("arbitrary",), vmem_limit_bytes=40 * 1024 * 1024
        ),
        cost_estimate=pl.CostEstimate(
            flops=part_len * width, bytes_accessed=part_len * width, transcendentals=0
        ),
        name="unrotate",
    )(returned, *tables)


def finish_body(
    groups,
    mine,
    chained,
    r_ref,
    dt_ref,
    w_ref,
    x_ref,
    y_ref,
    f_ref,
    second_ref,
    gain_ref,
    gain_two_ref,
    bias_ref,
    *refs,
):
    out_ref, grad_ref, gain_sum, shift_sum, gain_two_sum, shift_two_sum = refs[chained:]
    width = groups * mine

    @pl.when(pl.program_id(0) == 0)
    def _():
        gain_sum[...] = jnp.zeros_like(gain_sum)
        shift_sum[...] = jnp.zeros_like(shift_sum)
        gain_two_sum[...] = jnp.zeros_like(gain_two_sum)
        shift_two_sum[...] = jnp.zeros_like(shift_two_sum)

    x = x_ref[...].astype(jnp.float32)
    context = jnp.concatenate([r_ref[g] for g in range(groups)], axis=1)
    attended = jnp.dot(
        context, w_ref[:, 3 * width : 4 * width], preferred_element_type=jnp.float32
    )
    out_ref[...] = (x + (attended + bias_ref[...]) + f_ref[...]).astype(jnp.bfloat16)
    dh = lax.dot_general(
        dt_ref[...], w_ref[:, : 3 * width], NT, preferred_element_type=jnp.float32
    )
    average = jnp.mean(x, axis=-1, keepdims=True)
    centered = x - average
    inverse = lax.rsqrt(jnp.mean(centered * centered, axis=-1, keepdims=True) + epsilon)
    xh = centered * inverse
    gain_sum[...] += jnp.sum(dh * xh, axis=0, keepdims=True)
    shift_sum[...] += jnp.sum(dh, axis=0, keepdims=True)
    dh_two = second_ref[...]
    gain_two_sum[...] += jnp.sum(dh_two * xh, axis=0, keepdims=True)
    shift_two_sum[...] += jnp.sum(dh_two, axis=0, keepdims=True)
    dg = dh * gain_ref[...] + dh_two * gain_two_ref[...]
    first = jnp.mean(dg, axis=-1, keepdims=True)
    second = jnp.mean(dg * xh, axis=-1, keepdims=True)
    grad_ref[...] = y_ref[...].astype(jnp.float32) + (dg - first - xh * second) * inverse


def finish(
    which, returned, grads, weights, hidden, upstream, contracted, second, gains, bias, chain
):
    groups, _, part_len, mine = returned.shape
    seqs, _, width = hidden.shape
    block = min(256, part_len)
    chain = tuple(chain)

    def row(size):
        return pl.BlockSpec((1, size), lambda j: (0, 0))

    tokens = pl.BlockSpec((None, block, width), lambda j: (which, j, 0))
    triple = pl.BlockSpec((block, 3 * width), lambda j: (j, 0))
    ordinary = 10

    def body(*refs):
        finish_body(groups, mine, len(chain), *refs)

    return pl.pallas_call(
        body,
        grid=(part_len // block,),
        in_specs=[
            pl.BlockSpec((groups, None, block, mine), lambda j: (0, 0, j, 0)),
            triple,
            pl.BlockSpec(weights.shape, lambda j: (0, 0)),
            tokens,
            tokens,
            tokens,
            tokens,
            row(width),
            row(width),
            row(width),
        ]
        + [pl.BlockSpec(memory_space=pl.ANY)] * len(chain),
        out_specs=[tokens, tokens] + [row(width)] * 4,
        out_shape=[
            jax.ShapeDtypeStruct((seqs, part_len, width), jnp.bfloat16),
            jax.ShapeDtypeStruct((seqs, part_len, width), jnp.float32),
        ]
        + [jax.ShapeDtypeStruct((1, width), jnp.float32)] * 4,
        input_output_aliases={ordinary + i: i for i in range(len(chain))},
        compiler_params=pltpu.CompilerParams(
            dimension_semantics=("arbitrary",), vmem_limit_bytes=56 * 1024 * 1024
        ),
        cost_estimate=pl.CostEstimate(
            flops=part_len * width, bytes_accessed=part_len * width, transcendentals=0
        ),
        name="finish",
    )(
        returned, grads, weights, hidden, upstream, contracted, second, *gains, bias, *chain
    )


def product(low_ref, grad_refs, context_refs, y_ref, tiles):
    step = pl.program_id(0)
    part_len = grad_refs[0].shape[0]

    def triple():
        return sum(
            jnp.dot(
                low_ref[:, i * part_len : (i + 1) * part_len],
                grad_ref[...],
                preferred_element_type=jnp.float32,
            )
            for i, grad_ref in enumerate(grad_refs)
        )

    def dense():
        return sum(
            jnp.dot(
                context_ref[...],
                y_ref[i * part_len : (i + 1) * part_len, :],
                preferred_element_type=jnp.float32,
            )
            for i, context_ref in enumerate(context_refs)
        )

    return step < 3 * tiles, triple, (step >= 3 * tiles) & (step < 4 * tiles), dense


def early_gradient_body(tiles, count, low_ref, y_ref, *refs):
    out_ref = refs[-1]
    is_triple, triple, is_dense, dense = product(
        low_ref, refs[:count], refs[count : 2 * count], y_ref, tiles
    )

    @pl.when(is_triple)
    def _():
        out_ref[...] = triple()

    @pl.when(is_dense)
    def _():
        out_ref[...] = dense()


def late_gradient_body(tiles, low_ref, y_ref, grad_ref, context_ref, early_ref, out_ref):
    is_triple, triple, is_dense, dense = product(
        low_ref, [grad_ref], [context_ref], y_ref, tiles
    )

    @pl.when(is_triple)
    def _():
        out_ref[...] = (early_ref[...] + triple()).astype(jnp.bfloat16)

    @pl.when(is_dense)
    def _():
        out_ref[...] = (early_ref[...] + dense()).astype(jnp.bfloat16)


def early_gradient(turned, upstream, grads, contexts):
    width = turned.shape[0]
    count = len(grads)
    part_len = grads[0].shape[0]
    tokens = count * part_len
    tile = 256
    tiles = width // tile

    def body(*refs):
        early_gradient_body(tiles, count, *refs)

    return pl.pallas_call(
        body,
        grid=(4 * tiles,),
        in_specs=[
            pl.BlockSpec((width, tokens), lambda n: (0, 0)),
            pl.BlockSpec((tokens, tile), lambda n: (0, jnp.clip(n - 3 * tiles, 0, tiles - 1))),
        ]
        + [pl.BlockSpec((part_len, tile), lambda n: (0, jnp.minimum(n, 3 * tiles - 1)))] * count
        + [pl.BlockSpec((width, part_len), lambda n: (0, 0))] * count,
        out_specs=pl.BlockSpec((width, tile), lambda n: (0, n)),
        out_shape=jax.ShapeDtypeStruct((width, 4 * width), jnp.float32),
        compiler_params=pltpu.CompilerParams(
            dimension_semantics=("arbitrary",), vmem_limit_bytes=40 * 1024 * 1024
        ),
        cost_estimate=pl.CostEstimate(
            flops=part_len * width, bytes_accessed=part_len * width, transcendentals=0
        ),
        name="early_gradient",
    )(turned, upstream, *grads, *contexts)


def late_gradient(turned, upstream, grad, context, early):
    width = turned.shape[0]
    part_len = grad.shape[0]
    last = turned.shape[1] // part_len - 1
    tile = 512
    tiles = width // tile

    def body(*refs):
        late_gradient_body(tiles, *refs)

    return pl.pallas_call(
        body,
        grid=(4 * tiles,),
        in_specs=[
            pl.BlockSpec((width, part_len), lambda n: (0, last)),
            pl.BlockSpec(
                (part_len, tile), lambda n: (last, jnp.clip(n - 3 * tiles, 0, tiles - 1))
            ),
            pl.BlockSpec((part_len, tile), lambda n: (0, jnp.minimum(n, 3 * tiles - 1))),
            pl.BlockSpec((width, part_len), lambda n: (0, 0)),
            pl.BlockSpec((width, tile), lambda n: (0, n)),
        ],
        out_specs=pl.BlockSpec((width, tile), lambda n: (0, n)),
        out_shape=jax.ShapeDtypeStruct((width, 4 * width), jnp.bfloat16),
        compiler_params=pltpu.CompilerParams(
            dimension_semantics=("arbitrary",), vmem_limit_bytes=40 * 1024 * 1024
        ),
        cost_estimate=pl.CostEstimate(
            flops=2 * width * width * part_len,
            bytes_accessed=24 * width * width,
            transcendentals=0,
        ),
        name="late_gradient",
    )(turned, upstream, grad, context, early)


def join_body(near_ref, small_ref, out_ref):
    out_ref[...] = near_ref[...]


def join(near, small):
    return pl.pallas_call(
        join_body,
        in_specs=[pl.BlockSpec(memory_space=pltpu.VMEM), pl.BlockSpec(memory_space=pl.ANY)],
        out_specs=pl.BlockSpec(memory_space=pltpu.VMEM),
        out_shape=jax.ShapeDtypeStruct(near.shape, near.dtype),
        name="join",
    )(near, small)


def after(value, *others):
    return lax.optimization_barrier((value, *others))[0]


def scatter_sum(values):
    return lax.psum_scatter(values, "dp", scatter_dimension=0, tiled=True)


def local(
    hidden_in,
    cotangent,
    first_gain,
    first_shift,
    triple_weight,
    triple_bias,
    dense_weight,
    dense_bias,
    second_gain,
    second_shift,
    expand_weight,
    expand_bias,
    contract_weight,
    contract_bias,
):
    axes = ("dp", "seq")
    devices = lax.axis_size("dp") * lax.axis_size("seq")
    groups = lax.axis_size("seq")
    seqs, part_len, width = hidden_in.shape
    tokens_here = seqs * part_len
    shard = triple_weight.shape[0]
    vectors = (
        first_gain,
        first_shift,
        triple_bias,
        dense_bias,
        second_gain,
        second_shift,
        expand_bias,
        contract_bias,
    )
    columns = [vector.reshape(shard, -1) for vector in vectors]
    used = sum(column.shape[1] for column in columns)
    padding = jnp.zeros((shard, 128 - used), jnp.bfloat16)
    w_near = lax.all_gather(
        jnp.concatenate([triple_weight, dense_weight, *columns, padding], axis=1),
        axes,
        axis=0,
        tiled=True,
    )
    stacked = w_near[:, 4 * width : 4 * width + used].astype(jnp.float32)
    whole = []
    offset = 0
    for column in columns:
        size = column.shape[1]
        whole.append(stacked[:, offset : offset + size].reshape(-1))
        offset += size
    gain_one, shift_one, b_triple, b_dense, gain_two, shift_two, b_expand, b_contract = whole
    far = jnp.concatenate([expand_weight, contract_weight.reshape(shard, -1)], axis=1)
    hidden = expand_weight.shape[1]
    far = lax.all_gather(after(far, w_near), "seq", axis=0, tiled=True)
    upstream = cotangent.reshape(tokens_here, width)
    low_one, low_two, turned_one = normalize(
        hidden_in.reshape(tokens_here, width),
        gain_one[None],
        shift_one[None],
        gain_two[None],
        shift_two[None],
    )
    positions = lax.axis_index("seq") * part_len + jnp.arange(part_len, dtype=jnp.int32)
    tables = rotary_tables(positions, width // groups)
    sent = [
        project(which, low_one, upstream, w_near, b_triple[None], tables, part_len, groups)
        for which in range(seqs)
    ]

    def exchange(values):
        return lax.all_to_all(values, "seq", split_axis=0, concat_axis=0, tiled=True)

    received_0 = exchange(sent[0])
    received_1 = exchange(sent[1])
    far = after(far, sent[0])
    w_expand = lax.all_gather(far[:, :hidden], "dp", axis=0, tiled=True)
    w_contract = lax.all_gather(far[:, hidden:].reshape(-1, width), "dp", axis=0, tiled=True)
    low_two = after(low_two, received_0, *sent)
    expanded = jnp.dot(low_two, w_expand, preferred_element_type=jnp.float32) + b_expand
    activated, pull_gelu = jax.vjp(lambda inner: jax.nn.gelu(inner, approximate=False), expanded)
    low_act = activated.astype(jnp.bfloat16)
    contracted = (
        jnp.dot(low_act, w_contract, preferred_element_type=jnp.float32) + b_contract
    )
    received_2 = exchange(after(sent[2], low_act, contracted))
    outcome_0 = attention(after(received_0, received_1, low_act, contracted))
    upstream_ffn = after(upstream, outcome_0)
    grad_act = jnp.einsum(
        "td,fd->tf", upstream_ffn, w_contract, preferred_element_type=jnp.float32
    )
    grad_expanded = pull_gelu(grad_act)[0].astype(jnp.bfloat16)
    grad_b_expand = jnp.sum(grad_expanded.astype(jnp.float32), axis=0)
    outcome_1 = attention(after(received_1, received_2, grad_expanded))
    returned_0 = exchange(after(outcome_0, grad_expanded))
    grad_w_contract = jnp.einsum(
        "tf,td->fd", after(low_act, outcome_1), upstream, preferred_element_type=jnp.float32
    ).astype(jnp.bfloat16)
    outcome_2 = attention(after(received_2, returned_0, grad_w_contract))
    returned_1 = exchange(after(outcome_1, grad_w_contract))
    grad_w_expand = jnp.einsum(
        "td,tf->df",
        low_two,
        after(grad_expanded, outcome_2),
        preferred_element_type=jnp.float32,
    ).astype(jnp.bfloat16)
    returned_2 = exchange(after(outcome_2, grad_w_expand))
    sum_w_contract = scatter_sum(after(grad_w_contract, returned_0))
    sum_w_expand = scatter_sum(after(grad_w_expand, returned_1))
    grad_second = jnp.einsum(
        "tf,df->td", after(grad_expanded, returned_1), w_expand, preferred_element_type=jnp.float32
    )
    grad_second = grad_second.reshape(seqs, part_len, width)
    upstream_total = jnp.sum(upstream.astype(jnp.float32), axis=0)
    contracted = contracted.reshape(seqs, part_len, width)
    returned = [returned_0, returned_1, returned_2]
    unrotated = [unrotate(each, tables) for each in returned[:-1]]
    early = early_gradient(
        turned_one, upstream, [each[0] for each in unrotated], [each[1] for each in unrotated]
    )
    chain = ()
    sums = []
    for which in range(seqs):
        here = returned[which]
        if which == seqs - 1:
            here = after(here, early, *chain)
            unrotated.append(unrotate(here, tables))
            near = late_gradient(turned_one, upstream, *unrotated[-1][:2], early)
            here = after(here, near)
        results = finish(
            which,
            here,
            unrotated[which][0],
            w_near,
            hidden_in,
            cotangent,
            contracted,
            grad_second,
            (gain_one[None], gain_two[None]),
            b_dense[None],
            chain,
        )
        chain = results[:2]
        sums.append((*results[2:], unrotated[which][2]))
    block_out, grad_input = chain
    totals = [sum(each[1:], each[0]) for each in zip(*sums)]
    totals += [upstream_total, grad_b_expand]
    totals = [total.reshape(devices, -1) for total in totals]
    sizes = [total.shape[1] for total in totals]
    small = lax.psum_scatter(
        jnp.concatenate(totals, axis=1), axes, scatter_dimension=0, tiled=True
    ).reshape(-1)
    near = scatter_sum(near)
    near = join(near, small)
    last = lax.psum_scatter(near, "seq", scatter_dimension=0, tiled=True).astype(jnp.float32)
    rows_here = near.shape[0]
    far = jnp.concatenate([sum_w_expand, sum_w_contract.reshape(rows_here, -1)], axis=1)
    far = lax.all_to_all(
        far.reshape(groups, -1, far.shape[1]), "seq", split_axis=0, concat_axis=0, tiled=True
    )
    out_w_expand = jnp.sum(far[:, :, :hidden].astype(jnp.float32), axis=0)
    out_w_contract = jnp.sum(far[:, :, hidden:].astype(jnp.float32), axis=0).reshape(-1, width)
    out_w_triple = last[:, : 3 * width]
    out_w_dense = last[:, 3 * width : 4 * width]
    pieces = []
    offset = 0
    for size in sizes:
        pieces.append(small[offset : offset + size])
        offset += size
    out_gain_one, out_shift_one, out_gain_two, out_shift_two, out_b_triple = pieces[:5]
    out_b_dense, out_b_expand = pieces[5:]
    out_b_contract = out_b_dense
    return (
        block_out,
        grad_input,
        out_gain_one,
        out_shift_one,
        out_w_triple,
        out_b_triple,
        out_w_dense,
        out_b_dense,
        out_gain_two,
        out_shift_two,
        out_w_expand,
        out_b_expand,
        out_w_contract,
        out_b_contract,
    )


def solution(mesh):
    placed = (
        P("dp", "seq", None),
        P("dp", "seq", None),
        P(("dp", "seq")),
        P(("dp", "seq")),
        P(("dp", "seq"), None),
        P(("dp", "seq")),
        P(("dp", "seq"), None),
        P(("dp", "seq")),
        P(("dp", "seq")),
        P(("dp", "seq")),
        P(("dp", "seq"), None),
        P(("dp", "seq")),
        P(("dp", "seq"), None),
        P(("dp", "seq")),
    )
    return jax.shard_map(
        local,
        mesh=mesh,
        in_specs=placed,
        out_specs=(
            P("dp", "seq", None),
            P("dp", "seq", None),
            P(("dp", "seq")),
            P(("dp", "seq")),
            P(("dp", "seq"), None),
            P(("dp", "seq")),
            P(("dp", "seq"), None),
            P(("dp", "seq")),
            P(("dp", "seq")),
            P(("dp", "seq")),
            P(("dp", "seq"), None),
            P(("dp", "seq")),
            P(("dp", "seq"), None),
            P(("dp", "seq")),
        ),
        check_vma=False,
    )
```
